32 devices in a mesh: expert: 4 (over z), dp: 4 (over y, core), replica: 2 (over x).
Axes of the slice: x: 2, y: 2, z: 4, core: 2. Of those that a mesh axis runs over, the one named last changes fastest.
Arguments:
- cotangent: bfloat16 [2, 4, 4, 128, 2048], P('replica', 'expert', 'dp'), may hold values from -0.5 to 0.5
- expert_ids: int32 [2, 4, 4, 128, 2], P('replica', 'expert', 'dp'), may hold values from 0 to 3, all different within a row; in each aligned block of 128 rows (0 to 127, 128 to 255, ..., all dimensions but the last counted through in order) at most 96 rows name the same one
- gate_values: float32 [2, 4, 4, 128, 2], P('replica', 'expert', 'dp'), may hold values from 0.1 to 1
- hidden_saved: bfloat16 [2, 4, 4, 4, 4, 24, 7168], P('replica', 'expert', 'dp'), may hold values from -6 to 6
- output_saved: bfloat16 [2, 4, 4, 4, 4, 24, 2048], P('replica', 'expert', 'dp'), may hold values from -6 to 6
- weights: bfloat16 [2, 4, 7168, 2048], P('replica', 'expert', 'dp'), may hold values from -6 to 6
- moment_one: bfloat16 [2, 4, 7168, 2048], P('replica', 'expert', 'dp'), may hold values from -4 to 4
- moment_two: bfloat16 [2, 4, 7168, 2048], P('replica', 'expert', 'dp'), may hold values from 0.19921875 to 2
- anchor: float32 [4, 1792, 2048], P('expert', 'dp'), may hold values from -6 to 6
- outer_moment: float32 [4, 1792, 2048], P('expert', 'dp'), may hold values from -2 to 2
Outputs:
- new_weights: bfloat16 [2, 4, 7168, 2048], P('replica', 'expert', 'dp')
- gate_grads: float32 [2, 4, 4, 128, 2], P('replica', 'expert', 'dp')
- grad_rms: float32 [2], P('replica')
The draws below stay inside these ranges and needn't reach their ends.
Inputs may be any that keep to these rules, and one draw needn't show every extreme that they name: `expert_ids`: each token names two different experts; among the 128 tokens of one device no expert is named more than 96 times, a bound that some block reaches.
All inputs are finite; a program needn't handle non-finite values.
Results may differ from the reference program's by a relative error of at most 0.0075.
Values may be sent and summed in bfloat16 or wider, within the bound.
A program may use at most 192 MiB of HBM per device.

```python
import math
import jax
import jax.numpy as jnp
import numpy as np
from jax import lax

D = 2048
FF = 7168
TOK_DEV = 128
EXPERTS = 4
MOST = 96
CAP = 24
FRAG = 1792
N_EXPERT = 4
N_DP = 4
N_REPLICA = 2


def block_levels(stream_key, dims, split, least, top_value):
    gain = 1.0
    for axis_at, shards_of in split:
        steps = jax.random.uniform(jax.random.fold_in(jax.random.fold_in(stream_key, 6), axis_at), (shards_of,), jnp.float32, least / len(split), top_value / len(split))
        gain = gain * jnp.repeat(jnp.exp(steps), dims[axis_at] // shards_of).reshape((-1,) + (1,) * (len(dims) - 1 - axis_at))
    return gain


def routed_block(rng, own, number, rows, amount, top, most, lean):
    sequence = jax.random.permutation(rng, amount)
    crowded, common = portions_of(amount, rows * top, most, lean, True), portions_of(amount, rows * top, most, lean, False)
    places = jnp.arange(amount)

    def named(tallies, rotation):
        used = int((tallies > 0).sum())
        fixed = max(1, used // 4)
        passed = fixed + (places - fixed + rotation * (used - fixed)) % max(1, amount - fixed)
        return jnp.zeros((amount,), jnp.int32).at[sequence[jnp.where(places < fixed, places, passed)]].set(jnp.asarray(tallies, jnp.int32))

    tallies = jnp.where(number % 4 == 0, named(crowded, number // 4), named(common, number - number // 4 - 1))
    mixed = jax.random.permutation(jax.random.fold_in(own, 3), amount)
    donor, sink = mixed[0:amount // 2 * 2:2], mixed[1:amount // 2 * 2:2]
    slack = jnp.minimum(tallies[donor] - 1, most - tallies[sink]) // 2
    slack = jnp.where((donor == sequence[0]) | (sink == sequence[0]) | (tallies[sink] == 0), 0, jnp.maximum(slack, 0))
    passed = jax.random.randint(jax.random.fold_in(own, 4), (amount // 2,), 0, 1 << 20) % (slack + 1)
    tallies = tallies.at[donor].add(-passed).at[sink].add(passed)
    items = jnp.searchsorted(jnp.cumsum(tallies), jnp.arange(rows * top), side="right").astype(jnp.int32)
    table = items.reshape(top, rows).T
    table = table[jax.random.permutation(jax.random.fold_in(own, 1), rows)]
    rotation = jax.random.randint(jax.random.fold_in(own, 2), (rows, 1), 0, top)
    return jnp.take_along_axis(table, (jnp.arange(top)[None, :] + rotation) % top, axis=1)


def portions_of(count, total, most, lean, full):
    weights = [(1 << 20) // math.isqrt(standing ** lean) + 1 for standing in range(1, count + 1)]
    largest = most if full else min(most, max(-(-total // count), total * weights[0] // sum(weights)))
    least = 1 if total - largest >= count - 1 else 0
    holding, surplus = [largest] + [least] * (count - 1), total - largest - least * (count - 1)
    while surplus > 0:
        free = [i for i in range(1, count) if holding[i] < largest] or [i for i in range(1, count) if holding[i] < most]
        mass, remaining = sum([weights[i] for i in free]), surplus
        for i in free:
            addition = min(most - holding[i], max(1, remaining * weights[i] // mass), surplus)
            holding[i] = holding[i] + addition
            surplus = surplus - addition
    return np.array(holding)


def normal_values(stream_key, extent, spread, most, cuts=(), kind=jnp.bfloat16):
    drawn = spread * jax.random.normal(stream_key, extent, jnp.float32)
    if cuts:
        drawn = drawn * block_levels(stream_key, extent, cuts, -0.22, 0.18)
    return jnp.clip(drawn, -most, most).astype(kind)


def setup_inputs(seed: int = 0) -> dict:
    splits = jax.random.split(jax.random.key(seed), 11)
    cotangent = normal_values(splits[0], (N_REPLICA, N_EXPERT, N_DP, TOK_DEV, D), 0.0625, 0.5, ((0, 2), (1, 4), (2, 4)))
    expert_ids_keys = jax.random.split(jax.random.fold_in(splits[1], 1), N_REPLICA * N_EXPERT * N_DP * TOK_DEV // TOK_DEV)
    expert_ids_turns = jax.random.permutation(jax.random.fold_in(splits[1], 3), N_REPLICA * N_EXPERT * N_DP * TOK_DEV // TOK_DEV)
    expert_ids = jax.vmap(lambda own, number: routed_block(jax.random.fold_in(splits[1], 2), own, number, TOK_DEV, EXPERTS, 2, MOST, 2))(expert_ids_keys, expert_ids_turns).reshape((N_REPLICA, N_EXPERT, N_DP, TOK_DEV, 2))
    gate_values = jnp.clip(0.1 + 0.9 * jax.random.uniform(splits[2], (N_REPLICA, N_EXPERT, N_DP, TOK_DEV, 2), jnp.float32) ** block_levels(splits[2], (N_REPLICA, N_EXPERT, N_DP, TOK_DEV, 2), ((0, 2), (1, 4), (2, 4)), -0.2, 0.2), 0.1, 1.0)
    hidden_saved = normal_values(splits[3], (N_REPLICA, EXPERTS, N_DP, N_EXPERT, N_DP, CAP, FF), 1.0, 6.0, ((0, 2), (1, 4), (2, 4)))
    output_saved = normal_values(splits[4], (N_REPLICA, EXPERTS, N_DP, N_EXPERT, N_DP, CAP, D), 1.0, 6.0, ((0, 2), (1, 4), (2, 4)))
    weights = normal_values(splits[5], (N_REPLICA, EXPERTS, FF, D), 1.0, 6.0, ((0, 2), (1, 4), (2, 4)))
    moment_one = normal_values(splits[6], (N_REPLICA, EXPERTS, FF, D), 0.5, 4.0, ((0, 2), (1, 4), (2, 4)))
    moment_two = jnp.clip(jnp.exp(math.log(2.0) - 2.306499 * jax.random.uniform(splits[7], (N_REPLICA, EXPERTS, FF, D), jnp.float32) ** block_levels(splits[7], (N_REPLICA, EXPERTS, FF, D), ((0, 2), (1, 4), (2, 4)), -0.2, 0.2)), 0.19921875, 2.0).astype(jnp.bfloat16)
    anchor = normal_values(splits[8], (EXPERTS, FRAG, D), 1.0, 6.0, ((0, 4), (1, 4)), jnp.float32)
    outer_moment = normal_values(splits[9], (EXPERTS, FRAG, D), 0.3, 2.0, ((0, 4), (1, 4)), jnp.float32)
    return dict(cotangent=cotangent, expert_ids=expert_ids, gate_values=gate_values, hidden_saved=hidden_saved, output_saved=output_saved, weights=weights, moment_one=moment_one, moment_two=moment_two, anchor=anchor, outer_moment=outer_moment)


beta_one = 0.9
beta_two = 0.95
epsilon = 1e-08
inner_rate = 0.3
weight_decay = 0.1
outer_rate = 0.7
nesterov_coef = 0.9

def slot_places(expert_ids):
    chosen = expert_ids.reshape(expert_ids.shape[:-2] + (-1,))
    onehot = (chosen[..., None] == jnp.arange(EXPERTS, dtype=jnp.int32)).astype(jnp.int32)
    before = jnp.cumsum(onehot, axis=-2) - onehot
    order_rank = lax.optimization_barrier(jnp.sum(before * onehot, axis=-1))
    return (chosen, order_rank % N_DP, order_rank // N_DP)

def expert_update(packed):
    hidden_e, slots_e, weight_e, first_e, second_e = packed

    def add_holder(summed, pair):
        hidden_rows, slot_rows = pair
        partial_term = jnp.dot(hidden_rows.reshape(-1, FF).astype(jnp.float32).T, slot_rows.reshape(-1, D).astype(jnp.float32), preferred_element_type=jnp.float32)
        partial_term = lax.optimization_barrier(partial_term.astype(jnp.bfloat16)).astype(jnp.float32)
        return (summed + partial_term, None)
    gradient, _ = lax.scan(add_holder, jnp.zeros((FF, D), jnp.float32), (hidden_e, slots_e))
    squares = jnp.sum(gradient * gradient)
    first_new = beta_one * first_e.astype(jnp.float32) + (1.0 - beta_one) * gradient
    second_new = beta_two * second_e.astype(jnp.float32) + (1.0 - beta_two) * gradient * gradient
    weight_old = weight_e.astype(jnp.float32)
    inner_new = weight_old - inner_rate * (first_new / (jnp.sqrt(second_new) + epsilon) + weight_decay * weight_old)
    return (inner_new.astype(jnp.bfloat16), squares)

def reference(cotangent, expert_ids, gate_values, hidden_saved, output_saved, weights, moment_one, moment_two, anchor, outer_moment):
    chosen, holder, slot_index = slot_places(expert_ids)
    replica_idx = jnp.arange(N_REPLICA, dtype=jnp.int32)[:, None, None, None]
    source_exp = jnp.arange(N_EXPERT, dtype=jnp.int32)[None, :, None, None]
    source_dp = jnp.arange(N_DP, dtype=jnp.int32)[None, None, :, None]
    picked = output_saved[replica_idx, chosen, holder, source_exp, source_dp, slot_index]
    picked = picked.reshape(N_REPLICA, N_EXPERT, N_DP, TOK_DEV, 2, D)
    upstream = cotangent.astype(jnp.float32)
    gate_grads = jnp.einsum('abctkd,abctd->abctk', picked.astype(jnp.float32), upstream)
    sends = (gate_values[..., None] * upstream[..., None, :]).astype(jnp.bfloat16)
    sends = sends.reshape(N_REPLICA, N_EXPERT, N_DP, 2 * TOK_DEV, D)
    slot_values = jnp.zeros(output_saved.shape, jnp.bfloat16)
    slot_values = slot_values.at[replica_idx, chosen, holder, source_exp, source_dp, slot_index].set(sends)
    inner_list = []
    rms_list = []
    for replica in range(N_REPLICA):
        inner_new, squares = lax.map(expert_update, (hidden_saved[replica], slot_values[replica], weights[replica], moment_one[replica], moment_two[replica]))
        inner_list.append(inner_new)
        rms_list.append(jnp.sqrt(jnp.sum(squares) / (EXPERTS * FF * D)))
    summed = jnp.zeros(anchor.shape, jnp.float32)
    for replica in range(N_REPLICA):
        summed = summed + (anchor - inner_list[replica][:, 0::4, :].astype(jnp.float32))
    average = summed / N_REPLICA
    momentum = nesterov_coef * outer_moment + average
    new_anchor = (anchor - outer_rate * (average + nesterov_coef * momentum)).astype(jnp.bfloat16)
    new_weights = jnp.stack([inner_list[replica].at[:, 0::4, :].set(new_anchor) for replica in range(N_REPLICA)])
    grad_rms = jnp.stack(rms_list).astype(jnp.float32)
    return (new_weights, gate_grads, grad_rms)
```

```python
import functools

import jax
import jax.numpy as jnp
from jax import lax
from jax.experimental import pallas as pl
from jax.experimental.pallas import tpu as pltpu
from jax.sharding import PartitionSpec as P

beta_one = 0.9
beta_two = 0.95
epsilon = 1e-08
inner_rate = 0.3
weight_decay = 0.1
outer_rate = 0.7
nesterov_coef = 0.9

MESH = pl.DeviceIdType.MESH
BF = jnp.bfloat16
F32 = jnp.float32


def kernel(
    dims,
    ids_ref, gates_ref, cot_ref, hid_ref, osv_ref, w_ref, m1_ref, m2_ref, anc_ref, om_ref,
    wbuf, gg_ref, rms_ref,
    hid, hidt, slots, sends, m1buf, m2buf, ancbuf, ombuf, osv, cot, meta,
    frag_send, frag_recv, tmp, gg_acc, sq_acc, msg_send, msg_recv,
    load_sem, part_sem, ao_sem, hs_sem, hr_sem, zs_sem, zr_sem, es_sem, ys_sem, yr_sem, ps_sem, pr_sem,
    xs_sem, xr_sem, ms_sem, mr_sem,
):
    n_exp, n_dp, n_rep, cap, rows, width, full, nj, chunks, relay, ring = dims
    dc = width // nj
    n_src = n_exp * n_dp
    per = n_src * cap
    group = n_dp * cap
    depth = n_dp * per
    n_y = n_dp // 2
    e = lax.axis_index("expert")
    d = lax.axis_index("dp")
    r = lax.axis_index("replica")
    me = e * n_dp + d
    core = lax.rem(d, 2)
    yy = d // 2
    partner = yy * 2 + 1 - core
    other = lax.rem(r + 1, n_rep)
    toks = ids_ref.shape[1]

    def mod(x, n):
        return lax.rem(x + 2 * n, n)

    up = 2 * (2 * e // n_exp) - 1
    is_end = (e == 0) | (e == n_exp - 1)
    home = e if relay else 0

    def source(k):
        if k < n_exp - 1:
            return e - k * up
        return jnp.where(is_end, e - k * up, e + up)

    def cols(j):
        return pl.ds(pl.multiple_of(j * dc, 128), dc)

    def remote(src, dst, ssem, rsem, to):
        return pltpu.make_async_remote_copy(
            src_ref=src, dst_ref=dst, send_sem=ssem, recv_sem=rsem,
            device_id=to, device_id_type=MESH,
        )

    def load(src, dst, sem):
        return pltpu.make_async_copy(src, dst, sem)

    cot_load = load(cot_ref, cot.at[home, 0], load_sem.at[0])
    cot_load.start()
    osv_load = load(osv_ref, osv, load_sem.at[1])

    erow = lax.broadcasted_iota(jnp.int32, (8 * ((n_exp + 7) // 8), toks), 0)
    earlier = (
        lax.broadcasted_iota(jnp.int32, (toks, toks), 0) < lax.broadcasted_iota(jnp.int32, (toks, toks), 1)
    ).astype(F32).astype(BF)
    shift = n_dp.bit_length() - 1
    both = ids_ref[...]
    counts = ((both[0:1] == erow).astype(F32) + (both[1:2] == erow).astype(F32)).astype(BF)
    ranks = jnp.dot(counts, earlier, preferred_element_type=F32)

    def place(ids):
        rank = jnp.sum(jnp.where(ids == erow, ranks, 0.0), axis=0, keepdims=True).astype(jnp.int32)
        return (ids * n_dp + (rank & (n_dp - 1))) * cap + (rank >> shift)

    own_place = (place(both[0:1]), place(both[1:2]))
    mine = jnp.concatenate(
        [own_place[0].astype(F32), own_place[1].astype(F32), gates_ref[...], jnp.zeros((4, toks), F32)], axis=0
    )
    meta[pl.ds(home, 1), 0:1] = mine.reshape(1, 1, 8, toks)

    barrier = pltpu.get_barrier_semaphore()
    for k in range(1, n_src):
        to = mod(me + k, n_src)
        pl.semaphore_signal(barrier, inc=1, device_id={"expert": to // n_dp, "dp": lax.rem(to, n_dp)}, device_id_type=MESH)
    pl.semaphore_signal(barrier, inc=1, device_id={"replica": other}, device_id_type=MESH)
    pl.semaphore_wait(barrier, n_src)

    def y_piece(q, j, to):
        if j == nj:
            return remote(meta.at[home, 0], meta.at[home, q], ys_sem.at[q, j], yr_sem.at[q, j], {"dp": to})
        return remote(
            cot_ref.at[:, cols(j)], cot.at[home, q, :, cols(j)], ys_sem.at[q, j], yr_sem.at[q, j], {"dp": to}
        )

    y_sends = []
    for j in [nj] + list(range(nj)):
        for q in range(1, n_y):
            y_sends.append(y_piece(q, j, mod(yy + q, n_y) * 2 + core))
            y_sends[-1].start()

    def tokens(q, j, to, which):
        if j == nj:
            src, dst = meta.at[home, q], meta.at[e, q]
        else:
            dst = cot.at[e, q, :, cols(j)]
            src = cot_ref.at[:, cols(j)] if q == 0 else cot.at[home, q, :, cols(j)]
        return remote(src, dst, zs_sem.at[which, q, j], zr_sem.at[e, q, j], {"expert": to})

    def send_tokens(q, j):
        @pl.when(is_end)
        def _():
            tokens(q, j, e - 2 * up, 1).start()

        tokens(q, j, e - up, 0).start()

    if relay:
        send_tokens(0, nj)
        send_tokens(0, 0)

    def peer(k, sign):
        if k == n_dp:
            return partner
        return mod(yy + sign * ((k - 2) // 2 + 1), n_y) * 2 + lax.rem(k, 2)

    hid_own, hid_sends = {}, []

    def send_hidden(c):
        start, size = chunks[c]

        def part(to):
            return hid_ref.at[:, :, :, pl.ds(pl.multiple_of(to * rows + start, 128), size)]

        landing = hid.at[d, :, :, :, pl.ds(start, size)]
        for k in range(2, n_dp + 1):
            to = peer(k, 1)
            hid_sends.append(remote(part(to), landing, hs_sem.at[c, k - 2], hr_sem.at[c, d], {"dp": to}))
            hid_sends[-1].start()
        hid_own[c] = load(part(d), landing, load_sem.at[2 + c])
        hid_own[c].start()

    def part_loads(c):
        start, size = chunks[c]
        rows_c = pl.ds(start, size)
        return [
            load(src.at[rows_c], dst.at[rows_c], part_sem.at[i, c])
            for i, (src, dst) in enumerate([(w_ref, wbuf), (m1_ref, m1buf), (m2_ref, m2buf)])
        ]

    n_c = len(chunks)
    send_hidden(0)
    send_hidden(1)
    osv_load.start()
    for c in range(n_c):
        for l in part_loads(c):
            l.start()

    def table(pack, first, count):
        at = lax.broadcasted_iota(jnp.int32, (count, toks), 0)
        if isinstance(first, tuple):
            at = jnp.where(at < group, at + first[0], at + (first[1] - group))
        else:
            at = at + first
        at = at.astype(F32)
        hit0, hit1 = at == pack[0:1], at == pack[1:2]
        gate_slot = jnp.sum(
            jnp.where(hit0, pack[2:3], 0.0) + jnp.where(hit1, pack[3:4], 0.0), axis=1, keepdims=True
        )
        return (hit0.astype(F32) + hit1.astype(F32)).astype(BF), gate_slot

    def routed(a, q, j, first, count):
        lo, hi = j * dc, (j + 1) * dc
        pack = meta[pl.ds(a, 1), pl.ds(q, 1)].reshape(8, toks)
        onehot, gate_slot = table(pack, first, count)
        taken = cot[pl.ds(a, 1), pl.ds(q, 1), :, lo:hi].reshape(toks, dc)
        return (gate_slot * jnp.dot(onehot, taken, preferred_element_type=F32)).astype(BF)

    def keep(a, q, j, value):
        lo, hi = j * dc, (j + 1) * dc
        slots[:, pl.ds(a, 1), pl.ds(mod(yy - q, n_y), 1), pl.ds(core, 1), :, lo:hi] = (
            value.reshape(n_dp, 1, 1, 1, cap, dc)
        )

    end = jnp.where(up > 0, n_exp - 1, 0)

    def to_end(k, q, j):
        a = source(k)
        return remote(
            sends.at[k, q, :, :, cols(j)], slots.at[:, a, mod(yy - q, n_y), core, :, cols(j)],
            es_sem.at[k, q, j], zr_sem.at[a, q, j], {"expert": end},
        )

    def from_neighbour(k, q, j):
        a = source(k)
        here = slots.at[:, a, mod(yy - q, n_y), core, :, cols(j)]
        return remote(here, here, es_sem.at[0, q, j], zr_sem.at[a, q, j], {"expert": e - up})

    def z_plain(q, k, j, sending):
        a = mod(e + k, n_exp)
        return remote(
            sends.at[q, a, :, :, cols(j)],
            slots.at[:, e if sending else a, mod(yy - q, n_y), core, :, cols(j)],
            zs_sem.at[q, k - 1, j], zr_sem.at[e if sending else a, q, j], {"expert": a},
        )

    def event_y(j):
        for piece in ([nj, 0] if j == 0 else [j]):
            for q in range(1, n_y):
                y_piece(q, piece, mod(yy - q, n_y) * 2 + core).wait_recv()
                if relay:
                    send_tokens(q, piece)
        if relay and j + 1 < nj:
            send_tokens(0, j + 1)

    def event_relay(j, k):
        if not relay:
            lo, hi = j * dc, (j + 1) * dc
            if k == 0:
                for q in range(n_y):
                    sends[q, :, :, :, lo:hi] = routed(0, q, j, 0, per).reshape(n_exp, n_dp, cap, dc)
                    for s in range(1, n_exp):
                        z_plain(q, s, j, True).start()
                    keep(e, q, j, sends[q, pl.ds(e, 1), :, :, lo:hi].reshape(group, dc))
            return
        lo, hi = j * dc, (j + 1) * dc
        a = source(k)

        @pl.when(jnp.logical_not(is_end))
        def _():
            for q in range(n_y):
                if k > 0:
                    for piece in ([nj, 0] if j == 0 else [j]):
                        if piece == nj:
                            here = meta.at[a, q]
                        else:
                            here = cot.at[a, q, :, cols(piece)]
                        remote(here, here, zs_sem.at[0, q, piece], zr_sem.at[a, q, piece], {"expert": a}).wait_recv()
                if k < n_exp - 1:
                    value = routed(a, q, j, (e * group, end * group), 2 * group)
                    sends[k, q, :, :, lo:hi] = value[group:].reshape(n_dp, cap, dc)
                    to_end(k, q, j).start()
                    keep(a, q, j, value[:group])
                else:
                    keep(a, q, j, routed(a, q, j, e * group, group))

        if k == 0:
            @pl.when(is_end)
            def _():
                for q in range(n_y):
                    keep(a, q, j, routed(a, q, j, e * group, group))

    fwd = []

    def event_column(j):
        if relay:
            @pl.when(is_end)
            def _():
                for k in range(1, n_exp):
                    for q in range(n_y):
                        from_neighbour(k, q, j).wait_recv()
        else:
            for k in range(1, n_exp):
                for q in range(n_y):
                    z_plain(q, k, j, False).wait_recv()
        whole = slots.at[:, :, :, core, :, cols(j)]
        fwd.append(remote(whole, whole, ps_sem.at[j], pr_sem.at[j], {"dp": partner}))
        fwd[-1].start()

    def event_partner(j):
        lo, hi = j * dc, (j + 1) * dc
        got = slots.at[:, :, :, 1 - core, :, cols(j)]
        remote(got, got, ps_sem.at[j], pr_sem.at[j], {"dp": partner}).wait_recv()
        if j == 0:
            osv_load.wait()
        prod = (
            slots[pl.ds(d, 1), :, :, :, :, lo:hi].reshape(per, dc).astype(F32)
            * osv[:, :, :, lo:hi].reshape(per, dc).astype(F32)
        )
        part = prod[:, :128]
        for s in range(128, dc, 128):
            part = part + prod[:, s:s + 128]
        gg_acc[...] += part

    def event_turn(c):
        start, size = chunks[c]
        for k in range(n_dp + 1, 1, -1):
            if k > n_dp:
                h = d
                hid_own[c].wait()
            else:
                h = peer(k, -1)
                dst = hid.at[h, :, :, :, pl.ds(start, size)]
                remote(dst, dst, hs_sem.at[c, k - 2], hr_sem.at[c, h], {"dp": h}).wait_recv()
            for s in range(start, start + size, 128):
                block = hid[pl.ds(h, 1), :, :, :, s:s + 128].reshape(per, 128)
                hidt[s:s + 128, pl.ds(pl.multiple_of(h * per, 128), per)] = block.T
        for l in part_loads(c):
            l.wait()
        if c + 2 < n_c:
            send_hidden(c + 2)

    sq_acc[...] = jnp.zeros_like(sq_acc)
    gg_acc[...] = jnp.zeros_like(gg_acc)

    big = chunks[0][1]

    def spans(c, size):
        return (
            pl.ds(pl.multiple_of(c * big, 128), size) if isinstance(c, jax.Array) else pl.ds(chunks[c][0], size),
            pl.ds(pl.multiple_of(c * (big // 4), 32), size // 4) if isinstance(c, jax.Array)
            else pl.ds(chunks[c][0] // 4, size // 4),
        )

    def outer_loads(c, j, n, size):
        _, quarter = spans(c, size)
        slot = lax.rem(n, ring) if isinstance(n, jax.Array) else n % ring
        return slot, [
            load(src.at[quarter, cols(j)], dst.at[slot, pl.ds(0, size // 4)], ao_sem.at[i, slot])
            for i, (src, dst) in enumerate([(anc_ref, ancbuf), (om_ref, ombuf)])
        ]

    def exchange(c, j, size):
        _, quarter = spans(c, size)
        return remote(
            frag_send.at[quarter, cols(j)], frag_recv.at[quarter, cols(j)],
            xs_sem.at[c, j], xr_sem.at[c, j], {"replica": other},
        )

    def main(c, j, n, size):
        here, quarter = spans(c, size)
        for l in outer_loads(c, j, n, size)[1]:
            l.start()
        right = slots[:, :, :, :, :, cols(j)].reshape(depth, dc)
        g = jnp.dot(hidt[here, :], right, preferred_element_type=F32)
        sq_acc[...] += jnp.sum((g * g).reshape(size // 8, 8, dc), axis=0)
        first = beta_one * m1buf[here, cols(j)].astype(F32) + (1.0 - beta_one) * g
        second = beta_two * m2buf[here, cols(j)].astype(F32) + (1.0 - beta_two) * g * g
        old = wbuf[here, cols(j)].astype(F32)
        new = old - inner_rate * (first / (jnp.sqrt(second) + epsilon) + weight_decay * old)
        wbuf[here, cols(j)] = new.astype(BF)
        for s in range(0, dc, 128):
            tmp[s // 128, 0:size] = new[:, s:s + 128]
            frag_send[quarter, pl.ds(pl.multiple_of(j * dc + s, 128), 128)] = (
                tmp[s // 128, pl.ds(0, size // 4, stride=4), :].astype(BF)
            )
        exchange(c, j, size).start()

    def merge(c, j, n, size):
        here, quarter = spans(c, size)
        slot, outer = outer_loads(c, j, n, size)
        for l in outer:
            l.wait()
        exchange(c, j, size).wait_recv()
        start = ancbuf[pl.ds(slot, 1), 0:size // 4].reshape(size // 4, dc)
        moved = ombuf[pl.ds(slot, 1), 0:size // 4].reshape(size // 4, dc)
        summed = (start - frag_send[quarter, cols(j)].astype(F32)) + (start - frag_recv[quarter, cols(j)].astype(F32))
        average = summed / n_rep
        momentum = nesterov_coef * moved + average
        point = start - outer_rate * (average + nesterov_coef * momentum)
        for s in range(0, dc, 128):
            lanes = pl.ds(pl.multiple_of(j * dc + s, 128), 128)
            tmp[s // 128, 0:size] = wbuf[here, lanes].astype(F32)
            tmp[s // 128, pl.ds(0, size // 4, stride=4), :] = point[:, s:s + 128]
            wbuf[here, lanes] = tmp[s // 128, 0:size].astype(BF)

    def over(work, blocks):
        (c0, c1, j0, j1), base = blocks
        size = chunks[c0][1]
        if c1 - c0 == 1:
            cc = c0 if size != big else jnp.int32(c0)

            def step(i, _):
                work(cc, i, base + i - j0, size)
                return 0
            lax.fori_loop(j0, j1, step, 0)
        else:
            assert j1 - j0 == 1 and all(chunks[c] == (c * big, big) for c in range(c0, c1))

            def step(i, _):
                work(i, jnp.int32(j0), base + i - c0, size)
                return 0
            lax.fori_loop(c0, c1, step, 0)

    queue, count = [], 0

    def pending():
        return sum((b[1] - b[0]) * (b[3] - b[2]) for b, _ in queue)

    def event_block(*blocks):
        nonlocal count
        amount = (blocks[1] - blocks[0]) * (blocks[3] - blocks[2])
        while pending() + amount > ring:
            over(merge, queue.pop(0))
        queue.append((blocks, count))
        over(main, queue[-1])
        count += amount

    def event_merge(left):
        while len(queue) > left:
            over(merge, queue.pop(0))

    cot_load.wait()
    for name, *what in schedule(nj, chunks, n_exp, relay):
        {
            "y": event_y, "relay": event_relay, "column": event_column, "partner": event_partner,
            "turn": event_turn, "block": event_block, "merge": event_merge,
        }[name](*what)

    ones = jnp.ones((8, 128), F32)
    dots = lax.dot_general(
        ones, gg_acc[...], (((1,), (1,)), ((), ())), precision=lax.Precision.HIGHEST, preferred_element_type=F32
    )
    n_row = per // 128
    square = jnp.sum(jnp.sum(sq_acc[...], axis=1, keepdims=True), axis=0, keepdims=True)
    for s in range(n_row):
        msg_send[s:s + 1, :] = dots[0:1, s * 128:(s + 1) * 128]
    msg_send[n_row:, :] = jnp.broadcast_to(square, (msg_send.shape[0] - n_row, 128))
    m_sends = []
    for k in range(1, n_src):
        to = mod(me + k, n_src)
        m_sends.append(remote(
            msg_send, msg_recv.at[me], ms_sem.at[k - 1], mr_sem.at[me],
            {"expert": to // n_dp, "dp": lax.rem(to, n_dp)},
        ))
        m_sends[-1].start()
    msg_recv[pl.ds(me, 1)] = msg_send[...].reshape((1,) + msg_send.shape)
    event_merge(1)
    for k in range(1, n_src):
        src = mod(me + k, n_src)
        remote(
            msg_recv.at[src], msg_recv.at[src], ms_sem.at[k - 1], mr_sem.at[src],
            {"expert": src // n_dp, "dp": lax.rem(src, n_dp)},
        ).wait_recv()
    held = jnp.concatenate([msg_recv[:, s, :] for s in range(n_row)], axis=1)
    lane = lax.broadcasted_iota(jnp.int32, (per, toks), 0)
    device = lax.broadcasted_iota(jnp.int32, (n_src, toks), 0)
    for pick in range(2):
        holder = own_place[pick] // cap
        at = own_place[pick] - holder * cap + me * cap
        chosen = jnp.dot(
            held, (lane == at).astype(F32), precision=lax.Precision.HIGHEST, preferred_element_type=F32
        )
        value = jnp.sum(jnp.where(device == holder, chosen, 0.0), axis=0, keepdims=True)
        gg_ref[pick:pick + 1, :] = value / gates_ref[pick:pick + 1, :]
    squares = jnp.sum(msg_recv[:, n_row, :], axis=0, keepdims=True)
    rms_ref[...] = jnp.broadcast_to(jnp.sqrt(squares / (n_exp * full * width)), rms_ref.shape)
    event_merge(0)

    for copy in y_sends + hid_sends + fwd + m_sends:
        copy.wait_send()
    for c, (_, size) in enumerate(chunks):
        for j in range(nj):
            exchange(c, j, size).wait_send()
    if relay:
        for q in range(n_y):
            for j in range(nj + 1):
                tokens(q, j, e - up, 0).wait_send()

        @pl.when(is_end)
        def _():
            for q in range(n_y):
                for j in range(nj + 1):
                    tokens(q, j, e - 2 * up, 1).wait_send()

        @pl.when(jnp.logical_not(is_end))
        def _():
            for k in range(n_exp - 1):
                for q in range(n_y):
                    for j in range(nj):
                        to_end(k, q, j).wait_send()
    else:
        for q in range(n_y):
            for k in range(1, n_exp):
                for j in range(nj):
                    z_plain(q, k, j, True).wait_send()


def schedule(nj, chunks, n_exp, relay):
    if not relay or nj != 4 or len(chunks) != 8:
        order = [("y", j) for j in range(nj)] + [("relay", j, 0) for j in range(nj)]
        for j in range(nj):
            order += [("relay", j, k) for k in range(1, n_exp)] + [("column", j), ("partner", j)]
        for c in range(len(chunks)):
            order += [("turn", c), ("block", c, c + 1, 0, nj)]
        return order
    return [
        ("y", 0), ("relay", 0, 0), ("y", 1), ("relay", 1, 0), ("y", 2), ("y", 3),
        ("relay", 0, 1), ("relay", 0, 2), ("relay", 0, 3), ("column", 0), ("turn", 0), ("partner", 0),
        ("block", 0, 1, 0, 1),
        ("relay", 2, 0), ("relay", 1, 1), ("relay", 1, 2), ("relay", 1, 3),
        ("turn", 1), ("block", 1, 2, 0, 1),
        ("column", 1), ("partner", 1), ("block", 0, 2, 1, 2),
        ("relay", 2, 1), ("relay", 2, 2), ("relay", 2, 3),
        ("turn", 2), ("block", 2, 3, 0, 2),
        ("relay", 3, 0), ("column", 2), ("turn", 3), ("partner", 2), ("block", 3, 4, 0, 2), ("block", 0, 4, 2, 3),
        ("relay", 3, 1), ("relay", 3, 2), ("relay", 3, 3),
        ("column", 3), ("turn", 4), ("block", 4, 5, 0, 3), ("merge", 2), ("partner", 3),
        ("block", 0, 3, 3, 4), ("block", 3, 5, 3, 4),
        ("turn", 5), ("block", 5, 6, 0, 4), ("turn", 6), ("block", 6, 7, 0, 4), ("turn", 7), ("block", 7, 8, 0, 4),
    ]


def flush(w_ref, g_ref, r_ref, out_ref, gg_ref, rms_ref, sem):
    size = w_ref.shape[0] // sem.shape[0]
    copies = []
    for i in range(sem.shape[0]):
        part = pl.ds(i * size, size)
        copies.append(pltpu.make_async_copy(w_ref.at[part], out_ref.at[part], sem.at[i]))
        copies[-1].start()
    gg_ref[...] = g_ref[...]
    rms_ref[0] = r_ref[0, 0]
    for c in copies:
        c.wait()


def shards(
    cotangent, expert_ids, gate_values, hidden_saved, output_saved,
    weights, moment_one, moment_two, anchor, outer_moment,
):
    n_exp = lax.axis_size("expert")
    n_dp = lax.axis_size("dp")
    n_rep = lax.axis_size("replica")
    toks, width = cotangent.shape[3:]
    full = hidden_saved.shape[6]
    rows = full // n_dp
    ids = expert_ids.reshape(toks, 2).T
    gates = gate_values.reshape(toks, 2).T
    hidden = hidden_saved.reshape(hidden_saved.shape[3:])
    stored = output_saved.reshape(output_saved.shape[3:])
    cap = -(-hidden.shape[2] // 8) * 8
    if cap != hidden.shape[2]:
        more = ((0, 0), (0, 0), (0, cap - hidden.shape[2]), (0, 0))
        hidden, stored = jnp.pad(hidden, more), jnp.pad(stored, more)
    nj = 4
    dc = width // nj
    units = rows // 128
    sizes = [256] * ((units - 2) // 2) + [128] * (2 + (units - 2) % 2)
    chunks = [(sum(sizes[:c]), size) for c, size in enumerate(sizes)]
    relay = n_exp == 4
    ring = 8
    n_src = n_exp * n_dp
    n_y = n_dp // 2
    dims = (n_exp, n_dp, n_rep, cap, rows, width, full, nj, chunks, relay, ring)
    anyspace = pl.BlockSpec(memory_space=pl.ANY)
    vmem = pl.BlockSpec(memory_space=pltpu.VMEM)
    dma = pltpu.SemaphoreType.DMA
    per = n_src * cap
    updated, gg, rms = pl.pallas_call(
        functools.partial(kernel, dims),
        out_shape=(
            pltpu.VMEM((rows, width), BF),
            pltpu.VMEM((2, toks), F32),
            pltpu.VMEM((8, 128), F32),
        ),
        in_specs=[vmem, vmem] + [anyspace] * 8,
        out_specs=(vmem, vmem, vmem),
        scratch_shapes=[
            pltpu.VMEM((n_dp, n_exp, n_dp, cap, rows), BF),
            pltpu.VMEM((rows, n_dp * per), BF),
            pltpu.VMEM((n_dp, n_exp, n_y, 2, cap, width), BF),
            pltpu.VMEM((n_exp - 1, n_y, n_dp, cap, width) if relay else (n_y, n_exp, n_dp, cap, width), BF),
            pltpu.VMEM((rows, width), BF),
            pltpu.VMEM((rows, width), BF),
            pltpu.VMEM((ring, 64, dc), F32),
            pltpu.VMEM((ring, 64, dc), F32),
            pltpu.VMEM((n_exp, n_dp, cap, width), BF),
            pltpu.VMEM((n_exp if relay else 1, n_y, toks, width), BF),
            pltpu.VMEM((n_exp if relay else 1, n_y, 8, toks), F32),
            pltpu.VMEM((rows // 4, width), BF),
            pltpu.VMEM((rows // 4, width), BF),
            pltpu.VMEM((dc // 128, 256, 128), F32),
            pltpu.VMEM((per, 128), F32),
            pltpu.VMEM((8, dc), F32),
            pltpu.VMEM((8, 128), F32),
            pltpu.VMEM((n_src, 8, 128), F32),
            dma((2 + len(chunks),)), dma((3, len(chunks))), dma((2, ring)),
            dma((len(chunks), n_dp)), dma((len(chunks), n_dp)),
            dma((2, n_y, nj + 1) if relay else (n_y, n_exp, nj)), dma((n_exp, n_y, nj + 1)),
            dma((n_exp - 1, n_y, nj)), dma((n_y, nj + 1)), dma((n_y, nj + 1)),
            dma((nj,)), dma((nj,)), dma((len(chunks), nj)), dma((len(chunks), nj)),
            dma((n_src,)), dma((n_src,)),
        ],
        compiler_params=pltpu.CompilerParams(
            collective_id=0, has_side_effects=True, vmem_limit_bytes=62 * 1024 * 1024 - rows * width * 2
        ),
        name="step",
    )(
        ids, gates, cotangent.reshape(toks, width), hidden, stored,
        weights.reshape(rows, width), moment_one.reshape(rows, width), moment_two.reshape(rows, width),
        anchor.reshape(rows // 4, width), outer_moment.reshape(rows // 4, width),
    )
    updated, gg, rms = pl.pallas_call(
        flush,
        out_shape=(
            jax.ShapeDtypeStruct((rows, width), BF),
            jax.ShapeDtypeStruct((2, toks), F32),
            jax.ShapeDtypeStruct((1,), F32),
        ),
        in_specs=[vmem, vmem, vmem],
        out_specs=(anyspace, vmem, pl.BlockSpec(memory_space=pltpu.SMEM)),
        scratch_shapes=[dma((8,))],
        compiler_params=pltpu.CompilerParams(vmem_limit_bytes=4 * 1024 * 1024),
        name="flush",
    )(*[pltpu.with_memory_space_constraint(a, pltpu.VMEM) for a in (updated, gg, rms)])
    return (
        updated.reshape(1, 1, rows, width),
        gg.T.reshape(1, 1, 1, toks, 2),
        rms,
    )


def solution(mesh):
    return jax.shard_map(
        shards,
        mesh=mesh,
        in_specs=(
            P("replica", "expert", "dp", None, None),
            P("replica", "expert", "dp", None, None),
            P("replica", "expert", "dp", None, None),
            P("replica", "expert", "dp", None, None, None, None),
            P("replica", "expert", "dp", None, None, None, None),
            P("replica", "expert", "dp", None),
            P("replica", "expert", "dp", None),
            P("replica", "expert", "dp", None),
            P("expert", "dp", None),
            P("expert", "dp", None),
        ),
        out_specs=(
            P("replica", "expert", "dp", None),
            P("replica", "expert", "dp", None, None),
            P("replica"),
        ),
        check_vma=False,
    )
```

```python
import functools

import jax
import jax.numpy as jnp
from jax import lax
from jax.experimental import pallas as pl
from jax.experimental.pallas import tpu as pltpu
from jax.sharding import PartitionSpec as P

beta_one = 0.9
beta_two = 0.95
epsilon = 1e-08
inner_rate = 0.3
weight_decay = 0.1
outer_rate = 0.7
nesterov_coef = 0.9

MESH = pl.DeviceIdType.MESH
BF = jnp.bfloat16
F32 = jnp.float32


def kernel(
    dims,
    ids_ref, gates_ref, cot_ref, hid_ref, osv_ref, w_ref, m1_ref, m2_ref, anc_ref, om_ref,
    wbuf, gg_ref, rms_ref,
    hid, hidt, slots, sends, m1buf, m2buf, ancbuf, ombuf, osv, cot, meta,
    frag_send, frag_recv, tmp, gg_acc, sq_acc, msg_send, msg_recv,
    load_sem, part_sem, ao_sem, hs_sem, hr_sem, zs_sem, zr_sem, es_sem, ys_sem, yr_sem, ps_sem, pr_sem,
    xs_sem, xr_sem, ms_sem, mr_sem, far_sem,
):
    n_exp, n_dp, n_rep, cap, rows, width, full, nj, chunks, relay, ring = dims
    dc = width // nj
    n_src = n_exp * n_dp
    per = n_src * cap
    group = n_dp * cap
    depth = n_dp * per
    n_y = n_dp // 2
    e = lax.axis_index("expert")
    d = lax.axis_index("dp")
    r = lax.axis_index("replica")
    me = e * n_dp + d
    core = lax.rem(d, 2)
    yy = d // 2
    partner = yy * 2 + 1 - core
    other = lax.rem(r + 1, n_rep)
    toks = ids_ref.shape[1]

    def mod(x, n):
        return lax.rem(x + 2 * n, n)

    up = 2 * (2 * e // n_exp) - 1
    is_end = (e == 0) | (e == n_exp - 1)
    home = e if relay else 0

    def source(k):
        if k < n_exp - 1:
            return e - k * up
        return jnp.where(is_end, e - k * up, e + up)

    def cols(j):
        return pl.ds(pl.multiple_of(j * dc, 128), dc)

    def remote(src, dst, ssem, rsem, to):
        return pltpu.make_async_remote_copy(
            src_ref=src, dst_ref=dst, send_sem=ssem, recv_sem=rsem,
            device_id=to, device_id_type=MESH,
        )

    def load(src, dst, sem):
        return pltpu.make_async_copy(src, dst, sem)

    cot_load = load(cot_ref, cot.at[home, 0], load_sem.at[0])
    cot_load.start()
    osv_load = load(osv_ref, osv, load_sem.at[1])

    def part_loads(c):
        start, size = chunks[c]
        rows_c = pl.ds(start, size)
        return [
            load(src.at[rows_c], dst.at[rows_c], part_sem.at[i, c])
            for i, (src, dst) in enumerate([(w_ref, wbuf), (m1_ref, m1buf), (m2_ref, m2buf)])
        ]

    def start_part(c):
        if c < len(chunks):
            for l in part_loads(c):
                l.start()

    osv_load.start()
    start_part(0)
    start_part(1)

    erow = lax.broadcasted_iota(jnp.int32, (8 * ((n_exp + 7) // 8), toks), 0)
    earlier = (
        lax.broadcasted_iota(jnp.int32, (toks, toks), 0) < lax.broadcasted_iota(jnp.int32, (toks, toks), 1)
    ).astype(F32).astype(BF)
    shift = n_dp.bit_length() - 1
    both = ids_ref[...]
    counts = ((both[0:1] == erow).astype(F32) + (both[1:2] == erow).astype(F32)).astype(BF)
    ranks = jnp.dot(counts, earlier, preferred_element_type=F32)

    def place(ids):
        rank = jnp.sum(jnp.where(ids == erow, ranks, 0.0), axis=0, keepdims=True).astype(jnp.int32)
        return (ids * n_dp + (rank & (n_dp - 1))) * cap + (rank >> shift)

    own_place = (place(both[0:1]), place(both[1:2]))
    mine = jnp.concatenate(
        [own_place[0].astype(F32), own_place[1].astype(F32), gates_ref[...], jnp.zeros((4, toks), F32)], axis=0
    )
    meta[pl.ds(home, 1), 0:1] = mine.reshape(1, 1, 8, toks)

    barrier = pltpu.get_barrier_semaphore()

    def greet(to):
        pl.semaphore_signal(barrier, inc=1, device_id=to, device_id_type=MESH)

    greet({"replica": other})
    if relay:
        for k in range(1, n_dp):
            greet({"dp": mod(d + k, n_dp)})
        greet({"expert": e - up})

        @pl.when(jnp.logical_not(is_end))
        def _():
            greet({"expert": e + up})

        pl.semaphore_wait(barrier, n_dp + 2 - is_end.astype(jnp.int32))

        @pl.when(jnp.logical_not(is_end))
        def _():
            pl.semaphore_signal(far_sem, inc=1, device_id={"expert": e + up}, device_id_type=MESH)
    else:
        for k in range(1, n_src):
            to = mod(me + k, n_src)
            greet({"expert": to // n_dp, "dp": lax.rem(to, n_dp)})
        pl.semaphore_wait(barrier, n_src)

    def y_piece(q, j, to):
        if j == nj:
            return remote(meta.at[home, 0], meta.at[home, q], ys_sem.at[q, j], yr_sem.at[q, j], {"dp": to})
        return remote(
            cot_ref.at[:, cols(j)], cot.at[home, q, :, cols(j)], ys_sem.at[q, j], yr_sem.at[q, j], {"dp": to}
        )

    y_sends = []
    for j in [nj] + list(range(nj)):
        for q in range(1, n_y):
            y_sends.append(y_piece(q, j, mod(yy + q, n_y) * 2 + core))
            y_sends[-1].start()

    def tokens(q, j, to, which):
        if j == nj:
            src, dst = meta.at[home, q], meta.at[e, q]
        else:
            dst = cot.at[e, q, :, cols(j)]
            src = cot_ref.at[:, cols(j)] if q == 0 and j == 0 else cot.at[home, q, :, cols(j)]
        return remote(src, dst, zs_sem.at[which, q, j], zr_sem.at[e, q, j], {"expert": to})

    def send_tokens(q, j):
        @pl.when(is_end)
        def _():
            tokens(q, j, e - 2 * up, 1).start()

        tokens(q, j, e - up, 0).start()


    def peer(k, sign):
        if k == n_dp:
            return partner
        return mod(yy + sign * ((k - 2) // 2 + 1), n_y) * 2 + lax.rem(k, 2)

    hid_own, hid_sends = {}, []

    def send_hidden(c):
        start, size = chunks[c]

        def part(to):
            return hid_ref.at[:, :, :, pl.ds(pl.multiple_of(to * rows + start, 128), size)]

        landing = hid.at[d, :, :, :, pl.ds(start, size)]
        for k in range(2, n_dp + 1):
            to = peer(k, 1)
            hid_sends.append(remote(part(to), landing, hs_sem.at[c, k - 2], hr_sem.at[c, d], {"dp": to}))
            hid_sends[-1].start()
        hid_own[c] = load(part(d), landing, load_sem.at[2 + c])
        hid_own[c].start()

    n_c = len(chunks)
    for c in range(n_c):
        send_hidden(c)

    if relay:
        @pl.when(is_end)
        def _():
            pl.semaphore_wait(far_sem, 1)

        send_tokens(0, nj)
        send_tokens(0, 0)

    def table(pack, first, count):
        at = lax.broadcasted_iota(jnp.int32, (count, toks), 0)
        if isinstance(first, tuple):
            at = jnp.where(at < group, at + first[0], at + (first[1] - group))
        else:
            at = at + first
        at = at.astype(F32)
        hit0, hit1 = at == pack[0:1], at == pack[1:2]
        gate_slot = jnp.sum(
            jnp.where(hit0, pack[2:3], 0.0) + jnp.where(hit1, pack[3:4], 0.0), axis=1, keepdims=True
        )
        return (hit0.astype(F32) + hit1.astype(F32)).astype(BF), gate_slot

    def routed(a, q, j, first, count):
        lo, hi = j * dc, (j + 1) * dc
        pack = meta[pl.ds(a, 1), pl.ds(q, 1)].reshape(8, toks)
        onehot, gate_slot = table(pack, first, count)
        taken = cot[pl.ds(a, 1), pl.ds(q, 1), :, lo:hi].reshape(toks, dc)
        return (gate_slot * jnp.dot(onehot, taken, preferred_element_type=F32)).astype(BF)

    def keep(a, q, j, value):
        lo, hi = j * dc, (j + 1) * dc
        slots[:, pl.ds(a, 1), pl.ds(mod(yy - q, n_y), 1), pl.ds(core, 1), :, lo:hi] = (
            value.reshape(n_dp, 1, 1, 1, cap, dc)
        )

    end = jnp.where(up > 0, n_exp - 1, 0)

    def to_end(k, q, j):
        a = source(k)
        return remote(
            sends.at[k, q, :, :, cols(j)], slots.at[:, a, mod(yy - q, n_y), core, :, cols(j)],
            es_sem.at[k, q, j], zr_sem.at[a, q, j], {"expert": end},
        )

    def from_neighbour(k, q, j):
        a = source(k)
        here = slots.at[:, a, mod(yy - q, n_y), core, :, cols(j)]
        return remote(here, here, es_sem.at[0, q, j], zr_sem.at[a, q, j], {"expert": e - up})

    def z_plain(q, k, j, sending):
        a = mod(e + k, n_exp)
        return remote(
            sends.at[q, a, :, :, cols(j)],
            slots.at[:, e if sending else a, mod(yy - q, n_y), core, :, cols(j)],
            zs_sem.at[q, k - 1, j], zr_sem.at[e if sending else a, q, j], {"expert": a},
        )

    cot_load.wait()

    def event_y(j):
        for piece in ([nj, 0] if j == 0 else [j]):
            for q in range(1, n_y):
                y_piece(q, piece, mod(yy - q, n_y) * 2 + core).wait_recv()
                if relay:
                    send_tokens(q, piece)
        if relay and j + 1 < nj:
            send_tokens(0, j + 1)

    def event_relay(j, k):
        if not relay:
            lo, hi = j * dc, (j + 1) * dc
            if k == 0:
                for q in range(n_y):
                    sends[q, :, :, :, lo:hi] = routed(0, q, j, 0, per).reshape(n_exp, n_dp, cap, dc)
                    for s in range(1, n_exp):
                        z_plain(q, s, j, True).start()
                    keep(e, q, j, sends[q, pl.ds(e, 1), :, :, lo:hi].reshape(group, dc))
            return
        lo, hi = j * dc, (j + 1) * dc
        a = source(k)

        @pl.when(jnp.logical_not(is_end))
        def _():
            for q in range(n_y):
                if k > 0:
                    for piece in ([nj, 0] if j == 0 else [j]):
                        if piece == nj:
                            here = meta.at[a, q]
                        else:
                            here = cot.at[a, q, :, cols(piece)]
                        remote(here, here, zs_sem.at[0, q, piece], zr_sem.at[a, q, piece], {"expert": a}).wait_recv()
                if k < n_exp - 1:
                    value = routed(a, q, j, (e * group, end * group), 2 * group)
                    sends[k, q, :, :, lo:hi] = value[group:].reshape(n_dp, cap, dc)
                    to_end(k, q, j).start()
                    keep(a, q, j, value[:group])
                else:
                    keep(a, q, j, routed(a, q, j, e * group, group))

        if k == 0:
            @pl.when(is_end)
            def _():
                for q in range(n_y):
                    keep(a, q, j, routed(a, q, j, e * group, group))

    fwd = []

    def event_column(j):
        if relay:
            @pl.when(is_end)
            def _():
                for k in range(1, n_exp):
                    for q in range(n_y):
                        from_neighbour(k, q, j).wait_recv()
        else:
            for k in range(1, n_exp):
                for q in range(n_y):
                    z_plain(q, k, j, False).wait_recv()
        whole = slots.at[:, :, :, core, :, cols(j)]
        fwd.append(remote(whole, whole, ps_sem.at[j], pr_sem.at[j], {"dp": partner}))
        fwd[-1].start()

    def event_partner(j):
        lo, hi = j * dc, (j + 1) * dc
        got = slots.at[:, :, :, 1 - core, :, cols(j)]
        remote(got, got, ps_sem.at[j], pr_sem.at[j], {"dp": partner}).wait_recv()
        if j == 0:
            osv_load.wait()
        prod = (
            slots[pl.ds(d, 1), :, :, :, :, lo:hi].reshape(per, dc).astype(F32)
            * osv[:, :, :, lo:hi].reshape(per, dc).astype(F32)
        )
        part = prod[:, :128]
        for s in range(128, dc, 128):
            part = part + prod[:, s:s + 128]
        gg_acc[...] += part

    def event_turn(c):
        start, size = chunks[c]
        for k in range(n_dp + 1, 1, -1):
            if k > n_dp:
                h = d
                hid_own[c].wait()
            else:
                h = peer(k, -1)
                dst = hid.at[h, :, :, :, pl.ds(start, size)]
                remote(dst, dst, hs_sem.at[c, k - 2], hr_sem.at[c, h], {"dp": h}).wait_recv()
            for s in range(start, start + size, 128):
                block = hid[pl.ds(h, 1), :, :, :, s:s + 128].reshape(per, 128)
                hidt[s:s + 128, pl.ds(pl.multiple_of(h * per, 128), per)] = block.T
        for l in part_loads(c):
            l.wait()
        start_part(c + 2)

    sq_acc[...] = jnp.zeros_like(sq_acc)
    gg_acc[...] = jnp.zeros_like(gg_acc)

    big = chunks[0][1]

    def spans(c, size):
        return (
            pl.ds(pl.multiple_of(c * big, 128), size) if isinstance(c, jax.Array) else pl.ds(chunks[c][0], size),
            pl.ds(pl.multiple_of(c * (big // 4), 32), size // 4) if isinstance(c, jax.Array)
            else pl.ds(chunks[c][0] // 4, size // 4),
        )

    def outer_loads(c, j, n, size):
        _, quarter = spans(c, size)
        slot = lax.rem(n, ring) if isinstance(n, jax.Array) else n % ring
        return slot, [
            load(src.at[quarter, cols(j)], dst.at[slot, pl.ds(0, size // 4)], ao_sem.at[i, slot])
            for i, (src, dst) in enumerate([(anc_ref, ancbuf), (om_ref, ombuf)])
        ]

    def exchange(c, j, size):
        _, quarter = spans(c, size)
        return remote(
            frag_send.at[quarter, cols(j)], frag_recv.at[quarter, cols(j)],
            xs_sem.at[c, j], xr_sem.at[c, j], {"replica": other},
        )

    def main(c, j, n, size):
        here, quarter = spans(c, size)
        for l in outer_loads(c, j, n, size)[1]:
            l.start()
        right = slots[:, :, :, :, :, cols(j)].reshape(depth, dc)
        g = jnp.dot(hidt[here, :], right, preferred_element_type=F32)
        sq_acc[...] += jnp.sum((g * g).reshape(size // 8, 8, dc), axis=0)
        first = beta_one * m1buf[here, cols(j)].astype(F32) + (1.0 - beta_one) * g
        second = beta_two * m2buf[here, cols(j)].astype(F32) + (1.0 - beta_two) * g * g
        old = wbuf[here, cols(j)].astype(F32)
        new = old - inner_rate * (first / (second * lax.rsqrt(second) + epsilon) + weight_decay * old)
        wbuf[here, cols(j)] = new.astype(BF)
        for s in range(0, dc, 128):
            tmp[s // 128, 0:size] = new[:, s:s + 128]
            frag_send[quarter, pl.ds(pl.multiple_of(j * dc + s, 128), 128)] = (
                tmp[s // 128, pl.ds(0, size // 4, stride=4), :].astype(BF)
            )
        exchange(c, j, size).start()

    def merge(c, j, n, size):
        here, quarter = spans(c, size)
        slot, outer = outer_loads(c, j, n, size)
        for l in outer:
            l.wait()
        exchange(c, j, size).wait_recv()
        start = ancbuf[pl.ds(slot, 1), 0:size // 4].reshape(size // 4, dc)
        moved = ombuf[pl.ds(slot, 1), 0:size // 4].reshape(size // 4, dc)
        summed = (start - frag_send[quarter, cols(j)].astype(F32)) + (start - frag_recv[quarter, cols(j)].astype(F32))
        average = summed / n_rep
        momentum = nesterov_coef * moved + average
        point = start - outer_rate * (average + nesterov_coef * momentum)
        for s in range(0, dc, 128):
            lanes = pl.ds(pl.multiple_of(j * dc + s, 128), 128)
            tmp[s // 128, 0:size] = wbuf[here, lanes].astype(F32)
            tmp[s // 128, pl.ds(0, size // 4, stride=4), :] = point[:, s:s + 128]
            wbuf[here, lanes] = tmp[s // 128, 0:size].astype(BF)

    def over(work, blocks):
        (c0, c1, j0, j1), base = blocks
        size = chunks[c0][1]
        if c1 - c0 == 1:
            cc = c0 if size != big else jnp.int32(c0)

            def step(i, _):
                work(cc, i, base + i - j0, size)
                return 0
            lax.fori_loop(j0, j1, step, 0)
        else:
            assert j1 - j0 == 1 and all(chunks[c] == (c * big, big) for c in range(c0, c1))

            def step(i, _):
                work(i, jnp.int32(j0), base + i - c0, size)
                return 0
            lax.fori_loop(c0, c1, step, 0)

    queue, count = [], 0

    def pending():
        return sum((b[1] - b[0]) * (b[3] - b[2]) for b, _ in queue)

    def event_block(*blocks):
        nonlocal count
        amount = (blocks[1] - blocks[0]) * (blocks[3] - blocks[2])
        while pending() + amount > ring:
            over(merge, queue.pop(0))
        queue.append((blocks, count))
        over(main, queue[-1])
        count += amount

    def event_merge(left):
        while len(queue) > left:
            over(merge, queue.pop(0))

    for name, *what in schedule(nj, chunks, n_exp, relay):
        {
            "y": event_y, "relay": event_relay, "column": event_column, "partner": event_partner,
            "turn": event_turn, "block": event_block, "merge": event_merge,
        }[name](*what)

    ones = jnp.ones((8, 128), F32)
    dots = lax.dot_general(
        ones, gg_acc[...], (((1,), (1,)), ((), ())), precision=lax.Precision.HIGHEST, preferred_element_type=F32
    )
    n_row = per // 128
    square = jnp.sum(jnp.sum(sq_acc[...], axis=1, keepdims=True), axis=0, keepdims=True)
    for s in range(n_row):
        msg_send[s:s + 1, :] = dots[0:1, s * 128:(s + 1) * 128]
    msg_send[n_row:, :] = jnp.broadcast_to(square, (msg_send.shape[0] - n_row, 128))
    m_sends = []
    for k in range(1, n_src):
        to = mod(me + k, n_src)
        m_sends.append(remote(
            msg_send, msg_recv.at[me], ms_sem.at[k - 1], mr_sem.at[me],
            {"expert": to // n_dp, "dp": lax.rem(to, n_dp)},
        ))
        m_sends[-1].start()
    msg_recv[pl.ds(me, 1)] = msg_send[...].reshape((1,) + msg_send.shape)
    event_merge(1)
    for k in range(1, n_src):
        src = mod(me + k, n_src)
        remote(
            msg_recv.at[src], msg_recv.at[src], ms_sem.at[k - 1], mr_sem.at[src],
            {"expert": src // n_dp, "dp": lax.rem(src, n_dp)},
        ).wait_recv()
    held = jnp.concatenate([msg_recv[:, s, :] for s in range(n_row)], axis=1)
    lane = lax.broadcasted_iota(jnp.int32, (per, toks), 0)
    device = lax.broadcasted_iota(jnp.int32, (n_src, toks), 0)
    for pick in range(2):
        holder = own_place[pick] // cap
        at = own_place[pick] - holder * cap + me * cap
        chosen = jnp.dot(
            held, (lane == at).astype(F32), precision=lax.Precision.HIGHEST, preferred_element_type=F32
        )
        value = jnp.sum(jnp.where(device == holder, chosen, 0.0), axis=0, keepdims=True)
        gg_ref[pick:pick + 1, :] = value / gates_ref[pick:pick + 1, :]
    squares = jnp.sum(msg_recv[:, n_row, :], axis=0, keepdims=True)
    rms_ref[...] = jnp.broadcast_to(jnp.sqrt(squares / (n_exp * full * width)), rms_ref.shape)
    event_merge(0)

    for copy in y_sends + hid_sends + fwd + m_sends:
        copy.wait_send()
    for c, (_, size) in enumerate(chunks):
        for j in range(nj):
            exchange(c, j, size).wait_send()
    if relay:
        for q in range(n_y):
            for j in range(nj + 1):
                tokens(q, j, e - up, 0).wait_send()

        @pl.when(is_end)
        def _():
            for q in range(n_y):
                for j in range(nj + 1):
                    tokens(q, j, e - 2 * up, 1).wait_send()

        @pl.when(jnp.logical_not(is_end))
        def _():
            for k in range(n_exp - 1):
                for q in range(n_y):
                    for j in range(nj):
                        to_end(k, q, j).wait_send()
    else:
        for q in range(n_y):
            for k in range(1, n_exp):
                for j in range(nj):
                    z_plain(q, k, j, True).wait_send()


def schedule(nj, chunks, n_exp, relay):
    if not relay or nj != 4 or len(chunks) != 8:
        order = [("y", j) for j in range(nj)] + [("relay", j, 0) for j in range(nj)]
        for j in range(nj):
            order += [("relay", j, k) for k in range(1, n_exp)] + [("column", j), ("partner", j)]
        for c in range(len(chunks)):
            order += [("turn", c), ("block", c, c + 1, 0, nj)]
        return order
    return [
        ("y", 0), ("relay", 0, 0), ("y", 1), ("relay", 1, 0), ("y", 2), ("y", 3),
        ("relay", 0, 1), ("relay", 0, 2), ("relay", 0, 3), ("column", 0), ("turn", 0), ("partner", 0),
        ("block", 0, 1, 0, 1),
        ("relay", 2, 0), ("relay", 1, 1), ("relay", 1, 2), ("relay", 1, 3),
        ("turn", 1), ("block", 1, 2, 0, 1),
        ("column", 1), ("partner", 1), ("block", 0, 2, 1, 2),
        ("relay", 2, 1), ("relay", 2, 2), ("relay", 2, 3),
        ("turn", 2), ("block", 2, 3, 0, 2),
        ("relay", 3, 0), ("column", 2), ("turn", 3), ("partner", 2), ("block", 3, 4, 0, 2), ("block", 0, 4, 2, 3),
        ("relay", 3, 1), ("relay", 3, 2), ("relay", 3, 3),
        ("column", 3), ("turn", 4), ("block", 4, 5, 0, 3), ("merge", 2), ("partner", 3),
        ("block", 0, 3, 3, 4), ("block", 3, 5, 3, 4),
        ("turn", 5), ("block", 5, 6, 0, 4), ("turn", 6), ("block", 6, 7, 0, 4), ("turn", 7), ("block", 7, 8, 0, 4),
    ]


def flush(w_ref, g_ref, r_ref, out_ref, gg_ref, rms_ref, sem):
    size = w_ref.shape[0] // sem.shape[0]
    copies = []
    for i in range(sem.shape[0]):
        part = pl.ds(i * size, size)
        copies.append(pltpu.make_async_copy(w_ref.at[part], out_ref.at[part], sem.at[i]))
        copies[-1].start()
    gg_ref[...] = g_ref[...]
    rms_ref[0] = r_ref[0, 0]
    for c in copies:
        c.wait()


def shards(
    cotangent, expert_ids, gate_values, hidden_saved, output_saved,
    weights, moment_one, moment_two, anchor, outer_moment,
):
    n_exp = lax.axis_size("expert")
    n_dp = lax.axis_size("dp")
    n_rep = lax.axis_size("replica")
    toks, width = cotangent.shape[3:]
    full = hidden_saved.shape[6]
    rows = full // n_dp
    ids = expert_ids.reshape(toks, 2).T
    gates = gate_values.reshape(toks, 2).T
    hidden = hidden_saved.reshape(hidden_saved.shape[3:])
    stored = output_saved.reshape(output_saved.shape[3:])
    cap = -(-hidden.shape[2] // 8) * 8
    if cap != hidden.shape[2]:
        more = ((0, 0), (0, 0), (0, cap - hidden.shape[2]), (0, 0))
        hidden, stored = jnp.pad(hidden, more), jnp.pad(stored, more)
    nj = 4
    dc = width // nj
    units = rows // 128
    sizes = [256] * ((units - 2) // 2) + [128] * (2 + (units - 2) % 2)
    chunks = [(sum(sizes[:c]), size) for c, size in enumerate(sizes)]
    relay = n_exp == 4
    ring = 8
    n_src = n_exp * n_dp
    n_y = n_dp // 2
    dims = (n_exp, n_dp, n_rep, cap, rows, width, full, nj, chunks, relay, ring)
    anyspace = pl.BlockSpec(memory_space=pl.ANY)
    vmem = pl.BlockSpec(memory_space=pltpu.VMEM)
    dma = pltpu.SemaphoreType.DMA
    per = n_src * cap
    updated, gg, rms = pl.pallas_call(
        functools.partial(kernel, dims),
        out_shape=(
            pltpu.VMEM((rows, width), BF),
            pltpu.VMEM((2, toks), F32),
            pltpu.VMEM((8, 128), F32),
        ),
        in_specs=[vmem, vmem] + [anyspace] * 8,
        out_specs=(vmem, vmem, vmem),
        scratch_shapes=[
            pltpu.VMEM((n_dp, n_exp, n_dp, cap, rows), BF),
            pltpu.VMEM((rows, n_dp * per), BF),
            pltpu.VMEM((n_dp, n_exp, n_y, 2, cap, width), BF),
            pltpu.VMEM((n_exp - 1, n_y, n_dp, cap, width) if relay else (n_y, n_exp, n_dp, cap, width), BF),
            pltpu.VMEM((rows, width), BF),
            pltpu.VMEM((rows, width), BF),
            pltpu.VMEM((ring, 64, dc), F32),
            pltpu.VMEM((ring, 64, dc), F32),
            pltpu.VMEM((n_exp, n_dp, cap, width), BF),
            pltpu.VMEM((n_exp if relay else 1, n_y, toks, width), BF),
            pltpu.VMEM((n_exp if relay else 1, n_y, 8, toks), F32),
            pltpu.VMEM((rows // 4, width), BF),
            pltpu.VMEM((rows // 4, width), BF),
            pltpu.VMEM((dc // 128, 256, 128), F32),
            pltpu.VMEM((per, 128), F32),
            pltpu.VMEM((8, dc), F32),
            pltpu.VMEM((8, 128), F32),
            pltpu.VMEM((n_src, 8, 128), F32),
            dma((2 + len(chunks),)), dma((3, len(chunks))), dma((2, ring)),
            dma((len(chunks), n_dp)), dma((len(chunks), n_dp)),
            dma((2, n_y, nj + 1) if relay else (n_y, n_exp, nj)), dma((n_exp, n_y, nj + 1)),
            dma((n_exp - 1, n_y, nj)), dma((n_y, nj + 1)), dma((n_y, nj + 1)),
            dma((nj,)), dma((nj,)), dma((len(chunks), nj)), dma((len(chunks), nj)),
            dma((n_src,)), dma((n_src,)), pltpu.SemaphoreType.REGULAR,
        ],
        compiler_params=pltpu.CompilerParams(
            collective_id=0, has_side_effects=True, vmem_limit_bytes=62 * 1024 * 1024 - rows * width * 2
        ),
        name="step",
    )(
        ids, gates, cotangent.reshape(toks, width), hidden, stored,
        weights.reshape(rows, width), moment_one.reshape(rows, width), moment_two.reshape(rows, width),
        anchor.reshape(rows // 4, width), outer_moment.reshape(rows // 4, width),
    )
    updated, gg, rms = pl.pallas_call(
        flush,
        out_shape=(
            jax.ShapeDtypeStruct((rows, width), BF),
            jax.ShapeDtypeStruct((2, toks), F32),
            jax.ShapeDtypeStruct((1,), F32),
        ),
        in_specs=[vmem, vmem, vmem],
        out_specs=(anyspace, vmem, pl.BlockSpec(memory_space=pltpu.SMEM)),
        scratch_shapes=[dma((8,))],
        compiler_params=pltpu.CompilerParams(vmem_limit_bytes=4 * 1024 * 1024),
        name="flush",
    )(*[pltpu.with_memory_space_constraint(a, pltpu.VMEM) for a in (updated, gg, rms)])
    return (
        updated.reshape(1, 1, rows, width),
        gg.T.reshape(1, 1, 1, toks, 2),
        rms,
    )


def solution(mesh):
    return jax.shard_map(
        shards,
        mesh=mesh,
        in_specs=(
            P("replica", "expert", "dp", None, None),
            P("replica", "expert", "dp", None, None),
            P("replica", "expert", "dp", None, None),
            P("replica", "expert", "dp", None, None, None, None),
            P("replica", "expert", "dp", None, None, None, None),
            P("replica", "expert", "dp", None),
            P("replica", "expert", "dp", None),
            P("replica", "expert", "dp", None),
            P("expert", "dp", None),
            P("expert", "dp", None),
        ),
        out_specs=(
            P("replica", "expert", "dp", None),
            P("replica", "expert", "dp", None, None),
            P("replica"),
        ),
        check_vma=False,
    )
```

```python
import functools

import jax
import jax.numpy as jnp
from jax import lax
from jax.experimental import pallas as pl
from jax.experimental.pallas import tpu as pltpu
from jax.sharding import PartitionSpec as P

beta_one = 0.9
beta_two = 0.95
epsilon = 1e-08
inner_rate = 0.3
weight_decay = 0.1
outer_rate = 0.7
nesterov_coef = 0.9

MESH = pl.DeviceIdType.MESH
BF = jnp.bfloat16
F32 = jnp.float32


def kernel(
    dims,
    ids_ref, gates_ref, cot_ref, hid_ref, osv_ref, w_ref, m1_ref, m2_ref, anc_ref, om_ref,
    wbuf, gg_ref, rms_ref,
    hid, hidt, slots, sends, m1buf, m2buf, ancbuf, ombuf, osv, cot, meta,
    frag_send, frag_recv, tmp, gg_acc, sq_acc, msg_send, msg_recv,
    load_sem, part_sem, ao_sem, hs_sem, hr_sem, zs_sem, zr_sem, es_sem, ys_sem, yr_sem, ps_sem, pr_sem,
    xs_sem, xr_sem, ms_sem, mr_sem, far_sem,
):
    n_exp, n_dp, n_rep, cap, rows, width, full, nj, chunks, relay, ring = dims
    dc = width // nj
    n_src = n_exp * n_dp
    per = n_src * cap
    group = n_dp * cap
    depth = n_dp * per
    n_y = n_dp // 2
    e = lax.axis_index("expert")
    d = lax.axis_index("dp")
    r = lax.axis_index("replica")
    me = e * n_dp + d
    core = lax.rem(d, 2)
    yy = d // 2
    partner = yy * 2 + 1 - core
    other = lax.rem(r + 1, n_rep)
    toks = ids_ref.shape[1]

    def mod(x, n):
        return lax.rem(x + 2 * n, n)

    up = 2 * (2 * e // n_exp) - 1
    is_end = (e == 0) | (e == n_exp - 1)
    home = e if relay else 0

    def source(k):
        if k < n_exp - 1:
            return e - k * up
        return jnp.where(is_end, e - k * up, e + up)

    def cols(j):
        return pl.ds(pl.multiple_of(j * dc, 128), dc)

    def remote(src, dst, ssem, rsem, to):
        return pltpu.make_async_remote_copy(
            src_ref=src, dst_ref=dst, send_sem=ssem, recv_sem=rsem,
            device_id=to, device_id_type=MESH,
        )

    def load(src, dst, sem):
        return pltpu.make_async_copy(src, dst, sem)

    cot_load = load(cot_ref, cot.at[home, 0], load_sem.at[0])
    cot_load.start()
    osv_load = load(osv_ref, osv, load_sem.at[1])

    def part_loads(c):
        start, size = chunks[c]
        rows_c = pl.ds(start, size)
        return [
            load(src.at[rows_c], dst.at[rows_c], part_sem.at[i, c])
            for i, (src, dst) in enumerate([(w_ref, wbuf), (m1_ref, m1buf), (m2_ref, m2buf)])
        ]

    def start_part(c):
        if c < len(chunks):
            for l in part_loads(c):
                l.start()

    osv_load.start()
    start_part(0)
    start_part(1)

    erow = lax.broadcasted_iota(jnp.int32, (8 * ((n_exp + 7) // 8), toks), 0)
    earlier = (
        lax.broadcasted_iota(jnp.int32, (toks, toks), 0) < lax.broadcasted_iota(jnp.int32, (toks, toks), 1)
    ).astype(F32).astype(BF)
    shift = n_dp.bit_length() - 1
    both = ids_ref[...]
    counts = ((both[0:1] == erow).astype(F32) + (both[1:2] == erow).astype(F32)).astype(BF)
    ranks = jnp.dot(counts, earlier, preferred_element_type=F32)

    def place(ids):
        rank = jnp.sum(jnp.where(ids == erow, ranks, 0.0), axis=0, keepdims=True).astype(jnp.int32)
        return (ids * n_dp + (rank & (n_dp - 1))) * cap + (rank >> shift)

    own_place = (place(both[0:1]), place(both[1:2]))
    mine = jnp.concatenate(
        [own_place[0].astype(F32), own_place[1].astype(F32), gates_ref[...], jnp.zeros((4, toks), F32)], axis=0
    )
    meta[pl.ds(home, 1), 0:1] = mine.reshape(1, 1, 8, toks)

    barrier = pltpu.get_barrier_semaphore()

    def greet(to):
        pl.semaphore_signal(barrier, inc=1, device_id=to, device_id_type=MESH)

    greet({"replica": other})
    if relay:
        for k in range(1, n_dp):
            greet({"dp": mod(d + k, n_dp)})
        greet({"expert": e - up})

        @pl.when(jnp.logical_not(is_end))
        def _():
            greet({"expert": e + up})

        pl.semaphore_wait(barrier, n_dp + 2 - is_end.astype(jnp.int32))

        @pl.when(jnp.logical_not(is_end))
        def _():
            pl.semaphore_signal(far_sem, inc=1, device_id={"expert": e + up}, device_id_type=MESH)
    else:
        for k in range(1, n_src):
            to = mod(me + k, n_src)
            greet({"expert": to // n_dp, "dp": lax.rem(to, n_dp)})
        pl.semaphore_wait(barrier, n_src)

    def y_piece(q, j, to):
        if j == nj:
            return remote(meta.at[home, 0], meta.at[home, q], ys_sem.at[q, j], yr_sem.at[q, j], {"dp": to})
        return remote(
            cot_ref.at[:, cols(j)], cot.at[home, q, :, cols(j)], ys_sem.at[q, j], yr_sem.at[q, j], {"dp": to}
        )

    y_sends = []
    for j in [nj] + list(range(nj)):
        for q in range(1, n_y):
            y_sends.append(y_piece(q, j, mod(yy + q, n_y) * 2 + core))
            y_sends[-1].start()

    def tokens(q, j, to, which):
        if j == nj:
            src, dst = meta.at[home, q], meta.at[e, q]
        else:
            dst = cot.at[e, q, :, cols(j)]
            src = cot_ref.at[:, cols(j)] if q == 0 and j == 0 else cot.at[home, q, :, cols(j)]
        return remote(src, dst, zs_sem.at[which, q, j], zr_sem.at[e, q, j], {"expert": to})

    def send_tokens(q, j):
        @pl.when(is_end)
        def _():
            tokens(q, j, e - 2 * up, 1).start()

        tokens(q, j, e - up, 0).start()


    def peer(k, sign):
        if k == n_dp:
            return partner
        return mod(yy + sign * ((k - 2) // 2 + 1), n_y) * 2 + lax.rem(k, 2)

    hid_own, hid_sends = {}, []

    def send_hidden(c):
        start, size = chunks[c]

        def part(to):
            return hid_ref.at[:, :, :, pl.ds(pl.multiple_of(to * rows + start, 128), size)]

        landing = hid.at[d, :, :, :, pl.ds(start, size)]
        for k in range(2, n_dp + 1):
            to = peer(k, 1)
            hid_sends.append(remote(part(to), landing, hs_sem.at[c, k - 2], hr_sem.at[c, d], {"dp": to}))
            hid_sends[-1].start()
        hid_own[c] = load(part(d), landing, load_sem.at[2 + c])
        hid_own[c].start()

    n_c = len(chunks)
    for c in range(n_c):
        send_hidden(c)

    if relay:
        @pl.when(is_end)
        def _():
            pl.semaphore_wait(far_sem, 1)

        send_tokens(0, nj)
        send_tokens(0, 0)

    def table(pack, first, count):
        at = lax.broadcasted_iota(jnp.int32, (count, toks), 0)
        if isinstance(first, tuple):
            at = jnp.where(at < group, at + first[0], at + (first[1] - group))
        else:
            at = at + first
        at = at.astype(F32)
        hit0, hit1 = at == pack[0:1], at == pack[1:2]
        gate_slot = jnp.sum(
            jnp.where(hit0, pack[2:3], 0.0) + jnp.where(hit1, pack[3:4], 0.0), axis=1, keepdims=True
        )
        return (hit0.astype(F32) + hit1.astype(F32)).astype(BF), gate_slot

    def routed(a, q, j, first, count):
        lo, hi = j * dc, (j + 1) * dc
        pack = meta[pl.ds(a, 1), pl.ds(q, 1)].reshape(8, toks)
        onehot, gate_slot = table(pack, first, count)
        taken = cot[pl.ds(a, 1), pl.ds(q, 1), :, lo:hi].reshape(toks, dc)
        return (gate_slot * jnp.dot(onehot, taken, preferred_element_type=F32)).astype(BF)

    def keep(a, q, j, value):
        lo, hi = j * dc, (j + 1) * dc
        slots[:, pl.ds(a, 1), pl.ds(mod(yy - q, n_y), 1), pl.ds(core, 1), :, lo:hi] = (
            value.reshape(n_dp, 1, 1, 1, cap, dc)
        )

    end = jnp.where(up > 0, n_exp - 1, 0)

    def to_end(k, q, j):
        a = source(k)
        return remote(
            sends.at[k, q, :, :, cols(j)], slots.at[:, a, mod(yy - q, n_y), core, :, cols(j)],
            es_sem.at[k, q, j], zr_sem.at[a, q, j], {"expert": end},
        )

    def from_neighbour(k, q, j):
        a = source(k)
        here = slots.at[:, a, mod(yy - q, n_y), core, :, cols(j)]
        return remote(here, here, es_sem.at[0, q, j], zr_sem.at[a, q, j], {"expert": e - up})

    def z_plain(q, k, j, sending):
        a = mod(e + k, n_exp)
        return remote(
            sends.at[q, a, :, :, cols(j)],
            slots.at[:, e if sending else a, mod(yy - q, n_y), core, :, cols(j)],
            zs_sem.at[q, k - 1, j], zr_sem.at[e if sending else a, q, j], {"expert": a},
        )

    cot_load.wait()

    def event_y(j):
        for piece in ([nj, 0] if j == 0 else [j]):
            for q in range(1, n_y):
                y_piece(q, piece, mod(yy - q, n_y) * 2 + core).wait_recv()
                if relay:
                    send_tokens(q, piece)
        if relay and j + 1 < nj:
            send_tokens(0, j + 1)

    def event_relay(j, k):
        if not relay:
            lo, hi = j * dc, (j + 1) * dc
            if k == 0:
                for q in range(n_y):
                    sends[q, :, :, :, lo:hi] = routed(0, q, j, 0, per).reshape(n_exp, n_dp, cap, dc)
                    for s in range(1, n_exp):
                        z_plain(q, s, j, True).start()
                    keep(e, q, j, sends[q, pl.ds(e, 1), :, :, lo:hi].reshape(group, dc))
            return
        lo, hi = j * dc, (j + 1) * dc
        a = source(k)

        @pl.when(jnp.logical_not(is_end))
        def _():
            for q in range(n_y):
                if k > 0:
                    for piece in ([nj, 0] if j == 0 else [j]):
                        if piece == nj:
                            here = meta.at[a, q]
                        else:
                            here = cot.at[a, q, :, cols(piece)]
                        remote(here, here, zs_sem.at[0, q, piece], zr_sem.at[a, q, piece], {"expert": a}).wait_recv()
                if k < n_exp - 1:
                    value = routed(a, q, j, (e * group, end * group), 2 * group)
                    sends[k, q, :, :, lo:hi] = value[group:].reshape(n_dp, cap, dc)
                    to_end(k, q, j).start()
                    keep(a, q, j, value[:group])
                else:
                    keep(a, q, j, routed(a, q, j, e * group, group))

        if k == 0:
            @pl.when(is_end)
            def _():
                for q in range(n_y):
                    keep(a, q, j, routed(a, q, j, e * group, group))

    fwd = []

    def event_column(j):
        if relay:
            @pl.when(is_end)
            def _():
                for k in range(1, n_exp):
                    for q in range(n_y):
                        from_neighbour(k, q, j).wait_recv()
        else:
            for k in range(1, n_exp):
                for q in range(n_y):
                    z_plain(q, k, j, False).wait_recv()
        whole = slots.at[:, :, :, core, :, cols(j)]
        fwd.append(remote(whole, whole, ps_sem.at[j], pr_sem.at[j], {"dp": partner}))
        fwd[-1].start()

    def event_partner(j):
        lo, hi = j * dc, (j + 1) * dc
        got = slots.at[:, :, :, 1 - core, :, cols(j)]
        remote(got, got, ps_sem.at[j], pr_sem.at[j], {"dp": partner}).wait_recv()
        if j == 0:
            osv_load.wait()
        prod = (
            slots[pl.ds(d, 1), :, :, :, :, lo:hi].reshape(per, dc).astype(F32)
            * osv[:, :, :, lo:hi].reshape(per, dc).astype(F32)
        )
        part = prod[:, :128]
        for s in range(128, dc, 128):
            part = part + prod[:, s:s + 128]
        gg_acc[...] += part

    def event_turn(c):
        start, size = chunks[c]
        for k in range(n_dp + 1, 1, -1):
            if k > n_dp:
                h = d
                hid_own[c].wait()
            else:
                h = peer(k, -1)
                dst = hid.at[h, :, :, :, pl.ds(start, size)]
                remote(dst, dst, hs_sem.at[c, k - 2], hr_sem.at[c, h], {"dp": h}).wait_recv()
            for s in range(start, start + size, 128):
                block = hid[pl.ds(h, 1), :, :, :, s:s + 128].reshape(per, 128)
                hidt[s:s + 128, pl.ds(pl.multiple_of(h * per, 128), per)] = block.T
        for l in part_loads(c):
            l.wait()
        start_part(c + 2)

    sq_acc[...] = jnp.zeros_like(sq_acc)
    gg_acc[...] = jnp.zeros_like(gg_acc)

    big = chunks[0][1]

    def spans(c, size):
        return (
            pl.ds(pl.multiple_of(c * big, 128), size) if isinstance(c, jax.Array) else pl.ds(chunks[c][0], size),
            pl.ds(pl.multiple_of(c * (big // 4), 32), size // 4) if isinstance(c, jax.Array)
            else pl.ds(chunks[c][0] // 4, size // 4),
        )

    def outer_loads(c, j, n, size):
        _, quarter = spans(c, size)
        slot = lax.rem(n, ring) if isinstance(n, jax.Array) else n % ring
        return slot, [
            load(src.at[quarter, cols(j)], dst.at[slot, pl.ds(0, size // 4)], ao_sem.at[i, slot])
            for i, (src, dst) in enumerate([(anc_ref, ancbuf), (om_ref, ombuf)])
        ]

    def exchange(c, j, size):
        _, quarter = spans(c, size)
        return remote(
            frag_send.at[quarter, cols(j)], frag_recv.at[quarter, cols(j)],
            xs_sem.at[c, j], xr_sem.at[c, j], {"replica": other},
        )

    def main(c, j, n, size):
        here, quarter = spans(c, size)
        for l in outer_loads(c, j, n, size)[1]:
            l.start()
        right = slots[:, :, :, :, :, cols(j)].reshape(depth, dc)
        g = jnp.dot(hidt[here, :], right, preferred_element_type=F32)
        square = g * g
        sq_acc[...] += jnp.sum(square.reshape(size // 8, 8, dc), axis=0)
        first = (inner_rate * beta_one) * m1buf[here, cols(j)].astype(F32) + (inner_rate * (1.0 - beta_one)) * g
        second = beta_two * m2buf[here, cols(j)].astype(F32) + (1.0 - beta_two) * square
        old = wbuf[here, cols(j)].astype(F32)
        new = (1.0 - inner_rate * weight_decay) * old - first / (second * lax.rsqrt(second) + epsilon)
        wbuf[here, cols(j)] = new.astype(BF)
        for s in range(0, dc, 128):
            tmp[s // 128, 0:size] = new[:, s:s + 128]
            frag_send[quarter, pl.ds(pl.multiple_of(j * dc + s, 128), 128)] = (
                tmp[s // 128, pl.ds(0, size // 4, stride=4), :].astype(BF)
            )
        exchange(c, j, size).start()

    def merge(c, j, n, size):
        here, quarter = spans(c, size)
        slot, outer = outer_loads(c, j, n, size)
        for l in outer:
            l.wait()
        exchange(c, j, size).wait_recv()
        start = ancbuf[pl.ds(slot, 1), 0:size // 4].reshape(size // 4, dc)
        moved = ombuf[pl.ds(slot, 1), 0:size // 4].reshape(size // 4, dc)
        summed = (start - frag_send[quarter, cols(j)].astype(F32)) + (start - frag_recv[quarter, cols(j)].astype(F32))
        average = summed / n_rep
        momentum = nesterov_coef * moved + average
        point = start - outer_rate * (average + nesterov_coef * momentum)
        for s in range(0, dc, 128):
            lanes = pl.ds(pl.multiple_of(j * dc + s, 128), 128)
            tmp[s // 128, 0:size] = wbuf[here, lanes].astype(F32)
            tmp[s // 128, pl.ds(0, size // 4, stride=4), :] = point[:, s:s + 128]
            wbuf[here, lanes] = tmp[s // 128, 0:size].astype(BF)

    def over(work, blocks):
        (c0, c1, j0, j1), base = blocks
        size = chunks[c0][1]
        if c1 - c0 == 1:
            cc = c0 if size != big else jnp.int32(c0)

            def step(i, _):
                work(cc, i, base + i - j0, size)
                return 0
            lax.fori_loop(j0, j1, step, 0)
        else:
            assert j1 - j0 == 1 and all(chunks[c] == (c * big, big) for c in range(c0, c1))

            def step(i, _):
                work(i, jnp.int32(j0), base + i - c0, size)
                return 0
            lax.fori_loop(c0, c1, step, 0)

    queue, count = [], 0

    def pending():
        return sum((b[1] - b[0]) * (b[3] - b[2]) for b, _ in queue)

    def event_block(*blocks):
        nonlocal count
        amount = (blocks[1] - blocks[0]) * (blocks[3] - blocks[2])
        while pending() + amount > ring:
            over(merge, queue.pop(0))
        queue.append((blocks, count))
        over(main, queue[-1])
        count += amount

    def event_merge(left):
        while len(queue) > left:
            over(merge, queue.pop(0))

    for name, *what in schedule(nj, chunks, n_exp, relay):
        {
            "y": event_y, "relay": event_relay, "column": event_column, "partner": event_partner,
            "turn": event_turn, "block": event_block, "merge": event_merge,
        }[name](*what)

    ones = jnp.ones((8, 128), F32)
    dots = lax.dot_general(
        ones, gg_acc[...], (((1,), (1,)), ((), ())), precision=lax.Precision.HIGHEST, preferred_element_type=F32
    )
    n_row = per // 128
    square = jnp.sum(jnp.sum(sq_acc[...], axis=1, keepdims=True), axis=0, keepdims=True)
    for s in range(n_row):
        msg_send[s:s + 1, :] = dots[0:1, s * 128:(s + 1) * 128]
    msg_send[n_row:, :] = jnp.broadcast_to(square, (msg_send.shape[0] - n_row, 128))
    m_sends = []
    for k in range(1, n_src):
        to = mod(me + k, n_src)
        m_sends.append(remote(
            msg_send, msg_recv.at[me], ms_sem.at[k - 1], mr_sem.at[me],
            {"expert": to // n_dp, "dp": lax.rem(to, n_dp)},
        ))
        m_sends[-1].start()
    msg_recv[pl.ds(me, 1)] = msg_send[...].reshape((1,) + msg_send.shape)
    event_merge(0)
    for k in range(1, n_src):
        src = mod(me + k, n_src)
        remote(
            msg_recv.at[src], msg_recv.at[src], ms_sem.at[k - 1], mr_sem.at[src],
            {"expert": src // n_dp, "dp": lax.rem(src, n_dp)},
        ).wait_recv()
    held = jnp.concatenate([msg_recv[:, s, :] for s in range(n_row)], axis=1)
    lane = lax.broadcasted_iota(jnp.int32, (per, toks), 0)
    device = lax.broadcasted_iota(jnp.int32, (n_src, toks), 0)
    for pick in range(2):
        holder = own_place[pick] // cap
        at = own_place[pick] - holder * cap + me * cap
        chosen = jnp.dot(
            held, (lane == at).astype(F32), precision=lax.Precision.HIGHEST, preferred_element_type=F32
        )
        value = jnp.sum(jnp.where(device == holder, chosen, 0.0), axis=0, keepdims=True)
        gg_ref[pick:pick + 1, :] = value / gates_ref[pick:pick + 1, :]
    squares = jnp.sum(msg_recv[:, n_row, :], axis=0, keepdims=True)
    rms_ref[...] = jnp.broadcast_to(jnp.sqrt(squares / (n_exp * full * width)), rms_ref.shape)
    for copy in y_sends + hid_sends + fwd + m_sends:
        copy.wait_send()
    for c, (_, size) in enumerate(chunks):
        for j in range(nj):
            exchange(c, j, size).wait_send()
    if relay:
        for q in range(n_y):
            for j in range(nj + 1):
                tokens(q, j, e - up, 0).wait_send()

        @pl.when(is_end)
        def _():
            for q in range(n_y):
                for j in range(nj + 1):
                    tokens(q, j, e - 2 * up, 1).wait_send()

        @pl.when(jnp.logical_not(is_end))
        def _():
            for k in range(n_exp - 1):
                for q in range(n_y):
                    for j in range(nj):
                        to_end(k, q, j).wait_send()
    else:
        for q in range(n_y):
            for k in range(1, n_exp):
                for j in range(nj):
                    z_plain(q, k, j, True).wait_send()


def schedule(nj, chunks, n_exp, relay):
    if not relay or nj != 4 or len(chunks) != 8:
        order = [("y", j) for j in range(nj)] + [("relay", j, 0) for j in range(nj)]
        for j in range(nj):
            order += [("relay", j, k) for k in range(1, n_exp)] + [("column", j), ("partner", j)]
        for c in range(len(chunks)):
            order += [("turn", c), ("block", c, c + 1, 0, nj)]
        return order
    return [
        ("y", 0), ("relay", 0, 0), ("y", 1), ("relay", 1, 0), ("y", 2), ("y", 3),
        ("relay", 0, 1), ("relay", 0, 2), ("relay", 0, 3), ("column", 0), ("turn", 0), ("partner", 0),
        ("block", 0, 1, 0, 1),
        ("relay", 2, 0), ("relay", 1, 1), ("relay", 1, 2), ("relay", 1, 3),
        ("turn", 1), ("block", 1, 2, 0, 1),
        ("column", 1), ("partner", 1), ("block", 0, 2, 1, 2),
        ("relay", 2, 1), ("relay", 2, 2), ("relay", 2, 3),
        ("turn", 2), ("block", 2, 3, 0, 2),
        ("relay", 3, 0), ("column", 2), ("turn", 3), ("partner", 2), ("block", 3, 4, 0, 2), ("block", 0, 4, 2, 3),
        ("relay", 3, 1), ("relay", 3, 2), ("relay", 3, 3),
        ("column", 3), ("turn", 4), ("block", 4, 5, 0, 3), ("merge", 2), ("partner", 3),
        ("block", 0, 3, 3, 4), ("block", 3, 5, 3, 4),
        ("turn", 5), ("block", 5, 6, 0, 4), ("turn", 6), ("block", 6, 7, 0, 4), ("turn", 7), ("block", 7, 8, 0, 4),
    ]


def flush(w_ref, g_ref, r_ref, out_ref, gg_ref, rms_ref, sem):
    size = w_ref.shape[0] // sem.shape[0]
    copies = []
    for i in range(sem.shape[0]):
        part = pl.ds(i * size, size)
        copies.append(pltpu.make_async_copy(w_ref.at[part], out_ref.at[part], sem.at[i]))
        copies[-1].start()
    gg_ref[...] = g_ref[...]
    rms_ref[0] = r_ref[0, 0]
    for c in copies:
        c.wait()


def shards(
    cotangent, expert_ids, gate_values, hidden_saved, output_saved,
    weights, moment_one, moment_two, anchor, outer_moment,
):
    n_exp = lax.axis_size("expert")
    n_dp = lax.axis_size("dp")
    n_rep = lax.axis_size("replica")
    toks, width = cotangent.shape[3:]
    full = hidden_saved.shape[6]
    rows = full // n_dp
    ids = expert_ids.reshape(toks, 2).T
    gates = gate_values.reshape(toks, 2).T
    hidden = hidden_saved.reshape(hidden_saved.shape[3:])
    stored = output_saved.reshape(output_saved.shape[3:])
    cap = -(-hidden.shape[2] // 8) * 8
    if cap != hidden.shape[2]:
        more = ((0, 0), (0, 0), (0, cap - hidden.shape[2]), (0, 0))
        hidden, stored = jnp.pad(hidden, more), jnp.pad(stored, more)
    nj = 4
    dc = width // nj
    units = rows // 128
    sizes = [256] * ((units - 2) // 2) + [128] * (2 + (units - 2) % 2)
    chunks = [(sum(sizes[:c]), size) for c, size in enumerate(sizes)]
    relay = n_exp == 4
    ring = 8
    n_src = n_exp * n_dp
    n_y = n_dp // 2
    dims = (n_exp, n_dp, n_rep, cap, rows, width, full, nj, chunks, relay, ring)
    anyspace = pl.BlockSpec(memory_space=pl.ANY)
    vmem = pl.BlockSpec(memory_space=pltpu.VMEM)
    dma = pltpu.SemaphoreType.DMA
    per = n_src * cap
    updated, gg, rms = pl.pallas_call(
        functools.partial(kernel, dims),
        out_shape=(
            pltpu.VMEM((rows, width), BF),
            pltpu.VMEM((2, toks), F32),
            pltpu.VMEM((8, 128), F32),
        ),
        in_specs=[vmem, vmem] + [anyspace] * 8,
        out_specs=(vmem, vmem, vmem),
        scratch_shapes=[
            pltpu.VMEM((n_dp, n_exp, n_dp, cap, rows), BF),
            pltpu.VMEM((rows, n_dp * per), BF),
            pltpu.VMEM((n_dp, n_exp, n_y, 2, cap, width), BF),
            pltpu.VMEM((n_exp - 1, n_y, n_dp, cap, width) if relay else (n_y, n_exp, n_dp, cap, width), BF),
            pltpu.VMEM((rows, width), BF),
            pltpu.VMEM((rows, width), BF),
            pltpu.VMEM((ring, 64, dc), F32),
            pltpu.VMEM((ring, 64, dc), F32),
            pltpu.VMEM((n_exp, n_dp, cap, width), BF),
            pltpu.VMEM((n_exp if relay else 1, n_y, toks, width), BF),
            pltpu.VMEM((n_exp if relay else 1, n_y, 8, toks), F32),
            pltpu.VMEM((rows // 4, width), BF),
            pltpu.VMEM((rows // 4, width), BF),
            pltpu.VMEM((dc // 128, 256, 128), F32),
            pltpu.VMEM((per, 128), F32),
            pltpu.VMEM((8, dc), F32),
            pltpu.VMEM((8, 128), F32),
            pltpu.VMEM((n_src, 8, 128), F32),
            dma((2 + len(chunks),)), dma((3, len(chunks))), dma((2, ring)),
            dma((len(chunks), n_dp)), dma((len(chunks), n_dp)),
            dma((2, n_y, nj + 1) if relay else (n_y, n_exp, nj)), dma((n_exp, n_y, nj + 1)),
            dma((n_exp - 1, n_y, nj)), dma((n_y, nj + 1)), dma((n_y, nj + 1)),
            dma((nj,)), dma((nj,)), dma((len(chunks), nj)), dma((len(chunks), nj)),
            dma((n_src,)), dma((n_src,)), pltpu.SemaphoreType.REGULAR,
        ],
        compiler_params=pltpu.CompilerParams(
            collective_id=0, has_side_effects=True, vmem_limit_bytes=62 * 1024 * 1024 - rows * width * 2
        ),
        name="step",
    )(
        ids, gates, cotangent.reshape(toks, width), hidden, stored,
        weights.reshape(rows, width), moment_one.reshape(rows, width), moment_two.reshape(rows, width),
        anchor.reshape(rows // 4, width), outer_moment.reshape(rows // 4, width),
    )
    updated, gg, rms = pl.pallas_call(
        flush,
        out_shape=(
            jax.ShapeDtypeStruct((rows, width), BF),
            jax.ShapeDtypeStruct((2, toks), F32),
            jax.ShapeDtypeStruct((1,), F32),
        ),
        in_specs=[vmem, vmem, vmem],
        out_specs=(anyspace, vmem, pl.BlockSpec(memory_space=pltpu.SMEM)),
        scratch_shapes=[dma((8,))],
        compiler_params=pltpu.CompilerParams(vmem_limit_bytes=4 * 1024 * 1024),
        name="flush",
    )(*[pltpu.with_memory_space_constraint(a, pltpu.VMEM) for a in (updated, gg, rms)])
    return (
        updated.reshape(1, 1, rows, width),
        gg.T.reshape(1, 1, 1, toks, 2),
        rms,
    )


def solution(mesh):
    return jax.shard_map(
        shards,
        mesh=mesh,
        in_specs=(
            P("replica", "expert", "dp", None, None),
            P("replica", "expert", "dp", None, None),
            P("replica", "expert", "dp", None, None),
            P("replica", "expert", "dp", None, None, None, None),
            P("replica", "expert", "dp", None, None, None, None),
            P("replica", "expert", "dp", None),
            P("replica", "expert", "dp", None),
            P("replica", "expert", "dp", None),
            P("expert", "dp", None),
            P("expert", "dp", None),
        ),
        out_specs=(
            P("replica", "expert", "dp", None),
            P("replica", "expert", "dp", None, None),
            P("replica"),
        ),
        check_vma=False,
    )
```
